32 devices in a mesh: section: 2 (over core), ctx: 4 (over z), tp: 4 (over y, x).
Axes of the slice: x: 2, y: 2, z: 4, core: 2. Of those that a mesh axis runs over, the one named last changes fastest.
Arguments:
- queries: bfloat16 [2, 1024, 16384], P('section', 'ctx', 'tp'), may hold values from -32 to 32
- key_vectors: bfloat16 [2, 1024, 1024], P('section', ('ctx', 'tp')), may hold values from -32 to 32
- value_vectors: bfloat16 [2, 1024, 1024], P('section', ('ctx', 'tp')), may hold values from -6 to 6
- positions: int32 [1024], replicated, may hold values from 0 to 1023, each once
- residual: bfloat16 [1024, 16384], P(('ctx', 'tp')), may hold values from -3 to 3
Outputs:
- hidden_states: bfloat16 [2, 1024, 16384], P('section', ('ctx', 'tp'))
The draws below stay inside these ranges and needn't reach their ends.
All inputs are finite; a program needn't handle non-finite values.
Results may differ from the reference program's by a relative error of at most 0.0065.
Values may be sent and summed in bfloat16 or wider, within the bound.
A program may use at most 64 MiB of HBM per device.

```python
import math
import jax
import jax.numpy as jnp
from jax import lax

HEADS = 128
KV_HEADS = 8
HEAD_DIM = 128
SEQ = 1024
SECTIONS = 2


def draw_queries(key, part):
    own_key = jax.random.fold_in(key, 3)
    shape_full = (SECTIONS, SEQ, HEADS, HEAD_DIM)
    result = jnp.clip(2.0 * jax.random.normal(own_key, shape_full, jnp.float32), -12.0, 12.0)
    return result.reshape(SECTIONS, SEQ, HEADS * HEAD_DIM).astype(jnp.bfloat16)


def draw_key_vectors(key, part):
    own_key = jax.random.fold_in(key, 5)
    shape_full = (SECTIONS, SEQ, KV_HEADS, HEAD_DIM)
    result = jnp.clip(jax.random.normal(own_key, shape_full, jnp.float32), -6.0, 6.0)
    return result.reshape(SECTIONS, SEQ, KV_HEADS * HEAD_DIM).astype(jnp.bfloat16)


def level_of(rng, extent, cuts, least, top_value):
    def one(axis_at, parts):
        steps = jax.random.uniform(jax.random.fold_in(jax.random.fold_in(rng, 6), axis_at), (parts,), jnp.float32, least / len(cuts), top_value / len(cuts))
        return jnp.repeat(jnp.exp(steps), extent[axis_at] // parts).reshape((-1,) + (1,) * (len(extent) - axis_at - 1))

    loudness = one(*cuts[0])
    for cut in cuts[1:]:
        loudness = loudness * one(*cut)
    return loudness


def gaussian(key, extent, width, bound, shards=(), kind=jnp.bfloat16):
    values = jax.random.normal(key, extent, jnp.float32) * width
    if len(shards) > 0:
        values = level_of(key, extent, shards, -0.22, 0.18) * values
    return jnp.clip(values, min=-bound, max=bound).astype(kind)


def setup_inputs(seed: int = 0) -> dict:
    key_of = jax.random.split(jax.random.key(seed), 6)
    return {
        "queries": draw_queries(jax.random.fold_in(key_of[5], 71), 0),
        "key_vectors": draw_key_vectors(jax.random.fold_in(key_of[5], 71), 0),
        "value_vectors": gaussian(key_of[2], (SECTIONS, SEQ, KV_HEADS * HEAD_DIM), 1.0, 6.0, ((0, 2), (1, 16))),
        "positions": jax.random.permutation(key_of[3], SEQ).astype(jnp.int32),
        "residual": gaussian(key_of[4], (SEQ, HEADS * HEAD_DIM), 0.5, 3.0, ((0, 16),)),
    }


def head_attention(query_head, key_head, value_head, visible):
    scores = jnp.dot(query_head, key_head.T, preferred_element_type=jnp.float32) * (1.0 / math.sqrt(HEAD_DIM))
    scores = jnp.where(visible, scores, -jnp.inf)
    row_max = lax.optimization_barrier(jnp.max(scores, axis=1, keepdims=True))
    raised = jnp.exp(scores - row_max)
    totals = lax.optimization_barrier(jnp.sum(raised, axis=1, keepdims=True))
    weights = raised.astype(jnp.bfloat16)
    summed = jnp.dot(weights, value_head, preferred_element_type=jnp.float32)
    return (summed / totals).astype(jnp.bfloat16)

def section_attention(query_rows, key_rows, value_rows, visible):
    group_size = HEADS // KV_HEADS
    query_split = query_rows.reshape(SEQ, HEADS, HEAD_DIM)
    key_split = key_rows.reshape(SEQ, KV_HEADS, HEAD_DIM)
    value_split = value_rows.reshape(SEQ, KV_HEADS, HEAD_DIM)

    def one_head(head_index):
        kv_index = head_index // group_size
        query_head = lax.dynamic_index_in_dim(query_split, head_index, axis=1, keepdims=False)
        key_head = lax.dynamic_index_in_dim(key_split, kv_index, axis=1, keepdims=False)
        value_head = lax.dynamic_index_in_dim(value_split, kv_index, axis=1, keepdims=False)
        return head_attention(query_head, key_head, value_head, visible)
    outputs = lax.map(one_head, jnp.arange(HEADS, dtype=jnp.int32))
    return jnp.transpose(outputs, (1, 0, 2)).reshape(SEQ, HEADS * HEAD_DIM)

def reference(queries, key_vectors, value_vectors, positions, residual):
    visible = positions[None, :] <= positions[:, None]
    current = residual
    results = []
    for section_number in range(SECTIONS):
        attended = section_attention(queries[section_number], key_vectors[section_number], value_vectors[section_number], visible)
        attended = lax.optimization_barrier(attended)
        current = (current.astype(jnp.float32) + attended.astype(jnp.float32)).astype(jnp.bfloat16)
        current = lax.optimization_barrier(current)
        results.append(current)
    return jnp.stack(results)
```

```python
import functools
import math

import jax
import jax.numpy as jnp
from jax import lax
from jax.experimental import pallas as pl
from jax.experimental.pallas import tpu as pltpu
from jax.sharding import PartitionSpec as P

HEADS = 128
KV_HEADS = 8
HEAD_DIM = 128
MESH = pl.DeviceIdType.MESH
SCORE_SCALE = math.log2(math.e) / math.sqrt(HEAD_DIM)
HIDE = -1e30
TURN0 = 1
TURN1 = 2


def kernel(
    sizes,
    q_hbm,
    k_hbm,
    v_hbm,
    pos_ref,
    res_hbm,
    out_hbm,
    q_buf,
    k_ref,
    v_ref,
    stage,
    kvbuf,
    bias,
    att,
    rbuf,
    base,
    hbuf,
    in_sem,
    plane_send,
    plane_recv,
    far_send,
    far_recv,
    gate,
    a_send,
    a_recv,
    h_send,
    h_recv,
    out_sem,
):
    sections, ctx, tp, rows, own, kv_local, local_heads, chunk_heads = sizes
    group_size = HEADS // KV_HEADS
    width = local_heads * HEAD_DIM
    chunk = chunk_heads * HEAD_DIM
    chunks = local_heads // chunk_heads
    chunks_per_kv = chunks // kv_local
    seq = rows * ctx
    s = lax.axis_index("section")
    c = lax.axis_index("ctx")
    t = lax.axis_index("tp")
    me = c * tp + t

    def peer(j):
        return t ^ j if tp & (tp - 1) == 0 else lax.rem(t + j, tp)

    own_rows = pl.ds(pl.multiple_of(me * own, own), own)
    pair = 2 * HEAD_DIM

    k_copy = pltpu.make_async_copy(k_hbm, k_ref, in_sem.at[2])
    v_copy = pltpu.make_async_copy(v_hbm, v_ref, in_sem.at[3])
    k_copy.start()
    v_copy.start()

    barrier = pltpu.get_barrier_semaphore()

    @pl.loop(1, ctx * tp)
    def _(i):
        pl.semaphore_signal(
            barrier, inc=1, device_id=(s, lax.rem(c + i // tp, ctx), peer(lax.rem(i, tp))), device_id_type=MESH
        )

    @pl.when(s > 0)
    def _():
        pl.semaphore_signal(barrier, inc=1, device_id=(s - 1, c, t), device_id_type=MESH)

    @pl.when(s < sections - 1)
    def _():
        pl.semaphore_signal(barrier, inc=1, device_id=(s + 1, c, t), device_id_type=MESH)

    q_copy = pltpu.make_async_copy(q_hbm, q_buf, in_sem.at[0])
    q_copy.start()

    def res_copy(i):
        return pltpu.make_async_copy(
            res_hbm.at[:, pl.ds(pl.multiple_of(i * width, width), width)],
            base.at[i],
            in_sem.at[1],
        )

    @pl.when(s == 0)
    def _():
        @pl.loop(0, tp)
        def _(i):
            res_copy(i).start()

    def column(pt, g):
        head = pt * local_heads // group_size + g
        return pl.ds(pl.multiple_of(head * HEAD_DIM, HEAD_DIM), HEAD_DIM)

    k_copy.wait()
    v_copy.wait()
    for g in range(kv_local):
        @pl.loop(0, tp)
        def _(i):
            for part, src in enumerate((k_ref, v_ref)):
                stage[g, i, :, pl.ds(part * HEAD_DIM, HEAD_DIM)] = src[:, column(i, g)]

        kvbuf[g, own_rows, pl.ds(0, pair)] = stage[g, t]

    inner = jnp.minimum(s, 1) + jnp.minimum(sections - 1 - s, 1)
    pl.semaphore_wait(barrier, ctx * tp - 1 + inner)

    second = lax.rem(s, 2) == 1

    def kv_send(g, pc, pt, send_sem, recv_sem):
        return pltpu.make_async_remote_copy(
            src_ref=stage.at[g, pt],
            dst_ref=kvbuf.at[g, own_rows, pl.ds(0, pair)],
            send_sem=send_sem,
            recv_sem=recv_sem,
            device_id=(s, pc, pt),
            device_id_type=MESH,
        )

    def rows_moved(g, count, sem):
        moved = kvbuf.at[g, pl.ds(0, count), pl.ds(0, pair)]
        pltpu.make_async_copy(moved, moved, sem).wait()

    @pl.when(second)
    def _():
        pl.semaphore_wait(gate, 1)

    @pl.loop(1, ctx * tp)
    def _(i):
        kv_send(0, lax.rem(c + i // tp, ctx), peer(lax.rem(i, tp)), far_send.at[0], far_recv.at[0]).start()

    for g in range(1, kv_local):

        @pl.loop(1, tp)
        def _(i):
            kv_send(g, c, peer(i), plane_send.at[g], plane_recv.at[g]).start()

    for g in range(kv_local):
        kvbuf[g, :, pl.ds(pair, HEAD_DIM)] = jnp.ones((seq, HEAD_DIM), jnp.bfloat16)

    query_row = pos_ref[:, pl.ds(pl.multiple_of(c * rows, rows), rows)].astype(jnp.float32)
    query_pos = jnp.broadcast_to(query_row, (HEAD_DIM, rows)).T
    for i in range(seq // HEAD_DIM):
        cols = pl.ds(i * HEAD_DIM, HEAD_DIM)
        key_pos = pos_ref[:, cols].astype(jnp.float32)
        bias[:, cols] = jnp.where(key_pos <= query_pos, 0.0, HIDE)

    rows_moved(0, seq - own, far_send.at[0])

    @pl.when((lax.rem(s, 2) == 0) & (s < sections - 1))
    def _():
        pl.semaphore_signal(gate, inc=1, device_id=(lax.rem(s + 1, sections), c, t), device_id_type=MESH)

    def spread(g):
        block = kvbuf.at[g, pl.ds(pl.multiple_of(c * rows, rows), rows), pl.ds(0, pair)]

        @pl.loop(1, ctx)
        def _(j):
            pltpu.make_async_remote_copy(
                src_ref=block,
                dst_ref=block,
                send_sem=far_send.at[g],
                recv_sem=far_recv.at[g],
                device_id=(s, lax.rem(c + j, ctx), t),
                device_id_type=MESH,
            ).start()

    rows_moved(0, seq - own, far_recv.at[0])

    q_copy.wait()

    @pl.when(s == 0)
    def _():
        pltpu.make_async_copy(base, base, in_sem.at[1]).wait()

    def handoff(at, cols):
        return pltpu.make_async_remote_copy(
            src_ref=hbuf.at[:, :, cols],
            dst_ref=base.at[:, :, cols],
            send_sem=h_send,
            recv_sem=h_recv.at[at],
            device_id=(lax.rem(s + 1, sections), c, t),
            device_id_type=MESH,
        )

    def finish(at):
        cols = pl.ds(pl.multiple_of(at * chunk, chunk), chunk)
        landed = rbuf.at[pl.ds(0, tp - 1), :, cols]
        pltpu.make_async_copy(landed, landed, a_recv.at[at]).wait()

        @pl.when(s > 0)
        def _():
            arrived = base.at[:, :, cols]
            pltpu.make_async_copy(arrived, arrived, h_recv.at[at]).wait()

        hbuf[:, :, cols] = (
            base[:, :, cols].astype(jnp.float32) + rbuf[:, :, cols].astype(jnp.float32)
        ).astype(jnp.bfloat16)

        @pl.when(s < sections - 1)
        def _():
            handoff(at, cols).start()

        @pl.loop(0, tp)
        def _(i):
            place = pl.ds(pl.multiple_of(i * width + at * chunk, chunk), chunk)
            pltpu.make_async_copy(hbuf.at[i, :, cols], out_hbm.at[:, place], out_sem).start()

    lag = chunks // 2 + s
    turn = jnp.where(second, TURN1, TURN0)

    @pl.loop(0, kv_local)
    def _(g):
        @pl.when(g > 0)
        def _():
            rows_moved(g, seq - rows, far_recv.at[g])

        @pl.loop(0, chunks_per_kv)
        def _(n):
            at = g * chunks_per_kv + n
            def head(h):
                return pl.ds(pl.multiple_of(at * chunk + h * HEAD_DIM, HEAD_DIM), HEAD_DIM)

            def dots(h):
                return lax.dot_general(
                    q_buf[:, head(h)],
                    kvbuf[g, :, pl.ds(0, HEAD_DIM)],
                    (((1,), (1,)), ((), ())),
                    preferred_element_type=jnp.float32,
                )

            following = dots(0)
            for h in range(chunk_heads):
                scores = following * SCORE_SCALE + bias[...]
                if h + 1 < chunk_heads:
                    following = dots(h + 1)
                top = jnp.max(scores, axis=1, keepdims=True)
                weights = jnp.exp2(scores - top).astype(jnp.bfloat16)
                sums = jnp.dot(
                    weights,
                    kvbuf[g, :, pl.ds(HEAD_DIM, pair)],
                    preferred_element_type=jnp.float32,
                )
                att[:, head(h)] = (sums[:, :HEAD_DIM] / sums[:, HEAD_DIM:]).astype(jnp.bfloat16)
            cols = pl.ds(pl.multiple_of(at * chunk, chunk), chunk)

            @pl.loop(1, tp)
            def _(j):
                pt = peer(tp - j)
                pltpu.make_async_remote_copy(
                    src_ref=att.at[pl.ds(pl.multiple_of(pt * own, own), own), cols],
                    dst_ref=rbuf.at[t, :, cols],
                    send_sem=a_send,
                    recv_sem=a_recv.at[at],
                    device_id=(s, c, pt),
                    device_id_type=MESH,
                ).start()

            rbuf[t, :, cols] = att[pl.ds(pl.multiple_of(t * own, own), own), cols]

            @pl.when((g + 1 < kv_local) & (n == turn))
            def _():
                rows_moved(g + 1, (tp - 1) * own, plane_recv.at[g + 1])
                spread(g + 1)

            @pl.when(at >= lag)
            def _():
                finish(at - lag)

    @pl.loop(jnp.maximum(chunks - lag, 0), chunks)
    def _(at):
        finish(at)

    @pl.when(s < sections - 1)
    def _():
        pltpu.make_async_copy(hbuf, hbuf, h_send).wait()

    pltpu.make_async_copy(hbuf, hbuf, out_sem).wait()
    for g in range(1, kv_local):
        rows_moved(g, (tp - 1) * own, plane_send.at[g])
        rows_moved(g, seq - rows, far_send.at[g])

    sent = rbuf.at[pl.ds(0, tp - 1)]
    pltpu.make_async_copy(sent, sent, a_send).wait()


def body(queries, key_vectors, value_vectors, positions, residual):
    sections, ctx, tp = (lax.axis_size(name) for name in ("section", "ctx", "tp"))
    rows = queries.shape[1]
    own = key_vectors.shape[1]
    seq = positions.shape[0]
    local_heads = HEADS // tp
    kv_local = max(1, KV_HEADS // tp)
    chunk_heads = min(4, local_heads // kv_local)
    chunks = local_heads // chunk_heads
    width = local_heads * HEAD_DIM
    sizes = (sections, ctx, tp, rows, own, kv_local, local_heads, chunk_heads)
    half = jnp.bfloat16
    any_spec = pl.BlockSpec(memory_space=pl.ANY)
    hbm_spec = pl.BlockSpec(memory_space=pltpu.HBM)
    vmem_spec = pl.BlockSpec(memory_space=pltpu.VMEM)
    dma = pltpu.SemaphoreType.DMA
    hidden = pl.pallas_call(
        functools.partial(kernel, sizes),
        out_shape=jax.ShapeDtypeStruct((own, HEADS * HEAD_DIM), half),
        in_specs=[hbm_spec, hbm_spec, hbm_spec, vmem_spec, hbm_spec],
        out_specs=any_spec,
        scratch_shapes=[
            pltpu.VMEM((rows, width), half),
            pltpu.VMEM(key_vectors.shape[1:], half),
            pltpu.VMEM(value_vectors.shape[1:], half),
            pltpu.VMEM((kv_local, tp, own, 2 * HEAD_DIM), half),
            pltpu.VMEM((kv_local, seq, 3 * HEAD_DIM), half),
            pltpu.VMEM((rows, seq), jnp.float32),
            pltpu.VMEM((rows, width), half),
            pltpu.VMEM((tp, own, width), half),
            pltpu.VMEM((tp, own, width), half),
            pltpu.VMEM((tp, own, width), half),
            dma((4,)),
            dma((kv_local,)),
            dma((kv_local,)),
            dma((kv_local,)),
            dma((kv_local,)),
            pltpu.SemaphoreType.REGULAR,
            dma,
            dma((chunks,)),
            dma,
            dma((chunks,)),
            dma,
        ],
        compiler_params=pltpu.CompilerParams(
            collective_id=0, has_side_effects=True, vmem_limit_bytes=64 * 1024 * 1024
        ),
    )(queries[0], key_vectors[0], value_vectors[0], positions[None, :], residual)
    return hidden[None]


def solution(mesh):
    in_specs = (
        P("section", "ctx", "tp"),
        P("section", ("ctx", "tp"), None),
        P("section", ("ctx", "tp"), None),
        P(),
        P(("ctx", "tp"), None),
    )
    out_specs = P("section", ("ctx", "tp"), None)
    return jax.shard_map(body, mesh=mesh, in_specs=in_specs, out_specs=out_specs, check_vma=False)
```

```python
import functools
import math

import jax
import jax.numpy as jnp
from jax import lax
from jax.experimental import pallas as pl
from jax.experimental.pallas import tpu as pltpu
from jax.sharding import PartitionSpec as P

HEADS = 128
KV_HEADS = 8
HEAD_DIM = 128
MESH = pl.DeviceIdType.MESH
SCORE_SCALE = math.log2(math.e) / math.sqrt(HEAD_DIM)
HIDE = -1e30
TURN0 = 1
TURN1 = 2


def kernel(
    sizes,
    q_hbm,
    k_hbm,
    v_hbm,
    pos_hbm,
    res_hbm,
    out_ref,
    q_buf,
    pos_ref,
    kvbuf,
    bias,
    att,
    rbuf,
    base,
    in_sem,
    plane_send,
    plane_recv,
    far_send,
    far_recv,
    gate,
    a_send,
    a_recv,
    h_send,
    h_recv,
):
    sections, ctx, tp, rows, own, kv_local, local_heads, chunk_heads = sizes
    group_size = HEADS // KV_HEADS
    width = local_heads * HEAD_DIM
    chunk = chunk_heads * HEAD_DIM
    chunks = local_heads // chunk_heads
    chunks_per_kv = chunks // kv_local
    seq = rows * ctx
    s = lax.axis_index("section")
    c = lax.axis_index("ctx")
    t = lax.axis_index("tp")
    me = c * tp + t

    def peer(j):
        return t ^ j if tp & (tp - 1) == 0 else lax.rem(t + j, tp)

    own_rows = pl.ds(pl.multiple_of(me * own, own), own)
    pair = 2 * HEAD_DIM

    barrier = pltpu.get_barrier_semaphore()

    @pl.loop(1, ctx * tp)
    def _(i):
        pl.semaphore_signal(
            barrier, inc=1, device_id=(s, lax.rem(c + i // tp, ctx), peer(lax.rem(i, tp))), device_id_type=MESH
        )

    @pl.when(s > 0)
    def _():
        pl.semaphore_signal(barrier, inc=1, device_id=(s - 1, c, t), device_id_type=MESH)

    @pl.when(s < sections - 1)
    def _():
        pl.semaphore_signal(barrier, inc=1, device_id=(s + 1, c, t), device_id_type=MESH)

    pos_copy = pltpu.make_async_copy(pos_hbm, pos_ref, in_sem.at[3])
    pos_copy.start()
    q_copy = pltpu.make_async_copy(q_hbm, q_buf, in_sem.at[0])

    def res_copy(i):
        return pltpu.make_async_copy(
            res_hbm.at[:, pl.ds(pl.multiple_of(i * width, width), width)],
            base.at[i],
            in_sem.at[1],
        )

    def column(pt, g):
        head = pt * local_heads // group_size + g
        return pl.ds(pl.multiple_of(head * HEAD_DIM, HEAD_DIM), HEAD_DIM)

    inner = jnp.minimum(s, 1) + jnp.minimum(sections - 1 - s, 1)
    pl.semaphore_wait(barrier, ctx * tp - 1 + inner)

    second = lax.rem(s, 2) == 1

    def kv_parts(g, pt):
        for part, src in enumerate((k_hbm, v_hbm)):
            dst = kvbuf.at[g, own_rows, pl.ds(part * HEAD_DIM, HEAD_DIM)]
            yield src.at[:, column(pt, g)], dst

    def kv_send(g, pc, pt, send_sem, recv_sem):
        for src, dst in kv_parts(g, pt):
            pltpu.make_async_remote_copy(
                src_ref=src,
                dst_ref=dst,
                send_sem=send_sem,
                recv_sem=recv_sem,
                device_id=(s, pc, pt),
                device_id_type=MESH,
            ).start()

    def rows_moved(g, count, sem):
        moved = kvbuf.at[g, pl.ds(0, count), pl.ds(0, pair)]
        pltpu.make_async_copy(moved, moved, sem).wait()

    @pl.when(second)
    def _():
        pl.semaphore_wait(gate, 1)

    @pl.loop(1, ctx * tp)
    def _(i):
        kv_send(0, lax.rem(c + i // tp, ctx), peer(lax.rem(i, tp)), far_send.at[0], far_recv.at[0])

    for g in range(1, kv_local):

        @pl.loop(1, tp)
        def _(i):
            kv_send(g, c, peer(i), plane_send.at[g], plane_recv.at[g])

    for g in range(kv_local):
        for src, dst in kv_parts(g, t):
            pltpu.make_async_copy(src, dst, in_sem.at[2]).start()

    q_copy.start()

    @pl.when(s == 0)
    def _():
        @pl.loop(0, tp)
        def _(i):
            res_copy(i).start()

    for g in range(kv_local):
        kvbuf[g, :, pl.ds(pair, HEAD_DIM)] = jnp.ones((seq, HEAD_DIM), jnp.bfloat16)

    pos_copy.wait()
    query_row = pos_ref[:, pl.ds(pl.multiple_of(c * rows, rows), rows)].astype(jnp.float32)
    query_pos = jnp.broadcast_to(query_row, (HEAD_DIM, rows)).T
    for i in range(seq // HEAD_DIM):
        cols = pl.ds(i * HEAD_DIM, HEAD_DIM)
        key_pos = pos_ref[:, cols].astype(jnp.float32)
        bias[:, cols] = jnp.where(key_pos <= query_pos, 0.0, HIDE)

    rows_moved(0, seq - own, far_send.at[0])

    @pl.when((lax.rem(s, 2) == 0) & (s < sections - 1))
    def _():
        pl.semaphore_signal(gate, inc=1, device_id=(lax.rem(s + 1, sections), c, t), device_id_type=MESH)

    own_moved = kvbuf.at[:, pl.ds(0, own), pl.ds(0, pair)]
    pltpu.make_async_copy(own_moved, own_moved, in_sem.at[2]).wait()

    def spread(g):
        block = kvbuf.at[g, pl.ds(pl.multiple_of(c * rows, rows), rows), pl.ds(0, pair)]

        @pl.loop(1, ctx)
        def _(j):
            pltpu.make_async_remote_copy(
                src_ref=block,
                dst_ref=block,
                send_sem=far_send.at[g],
                recv_sem=far_recv.at[g],
                device_id=(s, lax.rem(c + j, ctx), t),
                device_id_type=MESH,
            ).start()

    rows_moved(0, seq - own, far_recv.at[0])

    q_copy.wait()

    @pl.when(s == 0)
    def _():
        pltpu.make_async_copy(base, base, in_sem.at[1]).wait()

    def place(i, at):
        return pl.ds(pl.multiple_of(i * width + at * chunk, chunk), chunk)

    def finish(at):
        cols = pl.ds(pl.multiple_of(at * chunk, chunk), chunk)
        landed = rbuf.at[pl.ds(0, tp - 1), :, cols]
        pltpu.make_async_copy(landed, landed, a_recv.at[at]).wait()

        @pl.when(s > 0)
        def _():
            arrived = base.at[:, :, cols]
            pltpu.make_async_copy(arrived, arrived, h_recv.at[at]).wait()

        @pl.loop(0, tp)
        def _(i):
            out_ref[:, place(i, at)] = (
                base[i, :, cols].astype(jnp.float32) + rbuf[i, :, cols].astype(jnp.float32)
            ).astype(jnp.bfloat16)

            @pl.when(s < sections - 1)
            def _():
                pltpu.make_async_remote_copy(
                    src_ref=out_ref.at[:, place(i, at)],
                    dst_ref=base.at[i, :, cols],
                    send_sem=h_send,
                    recv_sem=h_recv.at[at],
                    device_id=(lax.rem(s + 1, sections), c, t),
                    device_id_type=MESH,
                ).start()

    lag = chunks // 2 + s
    turn = jnp.where(second, TURN1, TURN0)

    @pl.loop(0, kv_local)
    def _(g):
        @pl.when(g > 0)
        def _():
            rows_moved(g, seq - rows, far_recv.at[g])

        @pl.loop(0, chunks_per_kv)
        def _(n):
            at = g * chunks_per_kv + n
            def head(h):
                return pl.ds(pl.multiple_of(at * chunk + h * HEAD_DIM, HEAD_DIM), HEAD_DIM)

            def dots(h):
                return lax.dot_general(
                    q_buf[:, head(h)],
                    kvbuf[g, :, pl.ds(0, HEAD_DIM)],
                    (((1,), (1,)), ((), ())),
                    preferred_element_type=jnp.float32,
                )

            following = dots(0)
            for h in range(chunk_heads):
                scores = following * SCORE_SCALE + bias[...]
                if h + 1 < chunk_heads:
                    following = dots(h + 1)
                top = jnp.max(scores, axis=1, keepdims=True)
                weights = jnp.exp2(scores - top).astype(jnp.bfloat16)
                sums = jnp.dot(
                    weights,
                    kvbuf[g, :, pl.ds(HEAD_DIM, pair)],
                    preferred_element_type=jnp.float32,
                )
                att[:, head(h)] = (sums[:, :HEAD_DIM] / sums[:, HEAD_DIM:]).astype(jnp.bfloat16)
            cols = pl.ds(pl.multiple_of(at * chunk, chunk), chunk)

            @pl.loop(1, tp)
            def _(j):
                pt = peer(tp - j)
                pltpu.make_async_remote_copy(
                    src_ref=att.at[pl.ds(pl.multiple_of(pt * own, own), own), cols],
                    dst_ref=rbuf.at[t, :, cols],
                    send_sem=a_send,
                    recv_sem=a_recv.at[at],
                    device_id=(s, c, pt),
                    device_id_type=MESH,
                ).start()

            rbuf[t, :, cols] = att[pl.ds(pl.multiple_of(t * own, own), own), cols]

            @pl.when((g + 1 < kv_local) & (n == turn))
            def _():
                rows_moved(g + 1, (tp - 1) * own, plane_recv.at[g + 1])
                spread(g + 1)

            @pl.when(at >= lag)
            def _():
                finish(at - lag)

    @pl.loop(jnp.maximum(chunks - lag, 0), chunks)
    def _(at):
        finish(at)

    @pl.when(s < sections - 1)
    def _():
        pltpu.make_async_copy(base, base, h_send).wait()

    for g in range(1, kv_local):
        rows_moved(g, (tp - 1) * own, plane_send.at[g])
        rows_moved(g, seq - rows, far_send.at[g])

    sent = rbuf.at[pl.ds(0, tp - 1)]
    pltpu.make_async_copy(sent, sent, a_send).wait()


def body(queries, key_vectors, value_vectors, positions, residual):
    sections, ctx, tp = (lax.axis_size(name) for name in ("section", "ctx", "tp"))
    rows = queries.shape[1]
    own = key_vectors.shape[1]
    seq = positions.shape[0]
    local_heads = HEADS // tp
    kv_local = max(1, KV_HEADS // tp)
    chunk_heads = min(4, local_heads // kv_local)
    chunks = local_heads // chunk_heads
    width = local_heads * HEAD_DIM
    sizes = (sections, ctx, tp, rows, own, kv_local, local_heads, chunk_heads)
    half = jnp.bfloat16
    hbm_spec = pl.BlockSpec(memory_space=pltpu.HBM)
    vmem_spec = pl.BlockSpec(memory_space=pltpu.VMEM)
    dma = pltpu.SemaphoreType.DMA
    hidden = pl.pallas_call(
        functools.partial(kernel, sizes),
        out_shape=pltpu.VMEM((own, HEADS * HEAD_DIM), half),
        in_specs=[hbm_spec] * 5,
        out_specs=vmem_spec,
        scratch_shapes=[
            pltpu.VMEM((rows, width), half),
            pltpu.VMEM((1, seq), jnp.int32),
            pltpu.VMEM((kv_local, seq, 3 * HEAD_DIM), half),
            pltpu.VMEM((rows, seq), jnp.float32),
            pltpu.VMEM((rows, width), half),
            pltpu.VMEM((tp, own, width), half),
            pltpu.VMEM((tp, own, width), half),
            dma((4,)),
            dma((kv_local,)),
            dma((kv_local,)),
            dma((kv_local,)),
            dma((kv_local,)),
            pltpu.SemaphoreType.REGULAR,
            dma,
            dma((chunks,)),
            dma,
            dma((chunks,)),
        ],
        compiler_params=pltpu.CompilerParams(
            collective_id=0, has_side_effects=True, vmem_limit_bytes=61 * 1024 * 1024
        ),
    )(queries[0], key_vectors[0], value_vectors[0], positions[None, :], residual)
    return hidden[None]


def solution(mesh):
    in_specs = (
        P("section", "ctx", "tp"),
        P("section", ("ctx", "tp"), None),
        P("section", ("ctx", "tp"), None),
        P(),
        P(("ctx", "tp"), None),
    )
    out_specs = P("section", ("ctx", "tp"), None)
    return jax.shard_map(body, mesh=mesh, in_specs=in_specs, out_specs=out_specs, check_vma=False)
```

```python
import functools
import math

import jax
import jax.numpy as jnp
from jax import lax
from jax.experimental import pallas as pl
from jax.experimental.pallas import tpu as pltpu
from jax.sharding import PartitionSpec as P

HEADS = 128
KV_HEADS = 8
HEAD_DIM = 128
MESH = pl.DeviceIdType.MESH
SCORE_SCALE = math.log2(math.e) / math.sqrt(HEAD_DIM)
HIDE = -1e30
FIRST = 2
TURN = 1


def kernel(
    sizes,
    q_hbm,
    k_hbm,
    v_hbm,
    pos_hbm,
    res_hbm,
    out_ref,
    q_buf,
    pos_ref,
    kvbuf,
    bias,
    att,
    rbuf,
    base,
    in_sem,
    plane_send,
    plane_recv,
    far_send,
    far_recv,
    gate,
    a_send,
    a_recv,
    h_send,
    h_recv,
):
    sections, ctx, tp, rows, own, kv_local, local_heads, chunk_heads = sizes
    group_size = HEADS // KV_HEADS
    width = local_heads * HEAD_DIM
    chunk = chunk_heads * HEAD_DIM
    chunks = local_heads // chunk_heads
    chunks_per_kv = chunks // kv_local
    seq = rows * ctx
    s = lax.axis_index("section")
    c = lax.axis_index("ctx")
    t = lax.axis_index("tp")
    me = c * tp + t

    def peer(j):
        return t ^ j if tp & (tp - 1) == 0 else lax.rem(t + j, tp)

    own_rows = pl.ds(pl.multiple_of(me * own, own), own)
    pair = 2 * HEAD_DIM

    barrier = pltpu.get_barrier_semaphore()

    @pl.loop(1, ctx * tp)
    def _(i):
        pl.semaphore_signal(
            barrier, inc=1, device_id=(s, lax.rem(c + i // tp, ctx), peer(lax.rem(i, tp))), device_id_type=MESH
        )

    @pl.when(s > 0)
    def _():
        pl.semaphore_signal(barrier, inc=1, device_id=(s - 1, c, t), device_id_type=MESH)

    @pl.when(s < sections - 1)
    def _():
        pl.semaphore_signal(barrier, inc=1, device_id=(s + 1, c, t), device_id_type=MESH)

    pos_copy = pltpu.make_async_copy(pos_hbm, pos_ref, in_sem.at[3])
    pos_copy.start()
    q_copy = pltpu.make_async_copy(q_hbm, q_buf, in_sem.at[0])

    def res_copy(i):
        return pltpu.make_async_copy(
            res_hbm.at[:, pl.ds(pl.multiple_of(i * width, width), width)],
            base.at[i],
            in_sem.at[1],
        )

    def column(pt, g):
        head = pt * local_heads // group_size + g
        return pl.ds(pl.multiple_of(head * HEAD_DIM, HEAD_DIM), HEAD_DIM)

    inner = jnp.minimum(s, 1) + jnp.minimum(sections - 1 - s, 1)
    pl.semaphore_wait(barrier, ctx * tp - 1 + inner)

    second = lax.rem(s, 2) == 1

    def kv_parts(g, pt):
        for part, src in enumerate((k_hbm, v_hbm)):
            dst = kvbuf.at[g, own_rows, pl.ds(part * HEAD_DIM, HEAD_DIM)]
            yield src.at[:, column(pt, g)], dst

    def kv_send(g, pc, pt, send_sem, recv_sem):
        for src, dst in kv_parts(g, pt):
            pltpu.make_async_remote_copy(
                src_ref=src,
                dst_ref=dst,
                send_sem=send_sem,
                recv_sem=recv_sem,
                device_id=(s, pc, pt),
                device_id_type=MESH,
            ).start()

    def rows_moved(g, count, sem):
        moved = kvbuf.at[g, pl.ds(0, count), pl.ds(0, pair)]
        pltpu.make_async_copy(moved, moved, sem).wait()

    @pl.when(second)
    def _():
        pl.semaphore_wait(gate, 1)

    @pl.loop(1, tp)
    def _(i):
        kv_send(0, c, peer(i), far_send.at[0], far_recv.at[0])

    @pl.loop(0, ctx * tp)
    def _(i):
        k = lax.rem(i, ctx)
        pc = jnp.where(2 * c < ctx, jnp.where(k == 0, ctx - 1, k - 1), jnp.where(k == 0, 0, ctx - k))

        @pl.when(pc != c)
        def _():
            kv_send(0, pc, peer(i // ctx), far_send.at[0], far_recv.at[0])


    for g in range(1, kv_local):

        @pl.loop(1, tp)
        def _(i):
            kv_send(g, c, peer(i), plane_send.at[g], plane_recv.at[g])

    for g in range(kv_local):
        for src, dst in kv_parts(g, t):
            pltpu.make_async_copy(src, dst, in_sem.at[2]).start()

    q_copy.start()

    @pl.when(s == 0)
    def _():
        @pl.loop(0, tp)
        def _(i):
            res_copy(i).start()

    for g in range(kv_local):
        kvbuf[g, :, pl.ds(pair, HEAD_DIM)] = jnp.ones((seq, HEAD_DIM), jnp.bfloat16)

    pos_copy.wait()
    query_row = pos_ref[:, pl.ds(pl.multiple_of(c * rows, rows), rows)].astype(jnp.float32)
    query_pos = jnp.broadcast_to(query_row, (HEAD_DIM, rows)).T
    for i in range(seq // HEAD_DIM):
        cols = pl.ds(i * HEAD_DIM, HEAD_DIM)
        key_pos = pos_ref[:, cols].astype(jnp.float32)
        bias[:, cols] = jnp.where(key_pos <= query_pos, 0.0, HIDE)

    rows_moved(0, seq - own, far_send.at[0])

    @pl.when((lax.rem(s, 2) == 0) & (s < sections - 1))
    def _():
        pl.semaphore_signal(gate, inc=1, device_id=(lax.rem(s + 1, sections), c, t), device_id_type=MESH)

    own_moved = kvbuf.at[:, pl.ds(0, own), pl.ds(0, pair)]
    pltpu.make_async_copy(own_moved, own_moved, in_sem.at[2]).wait()

    def spread(g):
        block = kvbuf.at[g, pl.ds(pl.multiple_of(c * rows, rows), rows), pl.ds(0, pair)]

        @pl.loop(1, ctx)
        def _(j):
            pltpu.make_async_remote_copy(
                src_ref=block,
                dst_ref=block,
                send_sem=far_send.at[g],
                recv_sem=far_recv.at[g],
                device_id=(s, lax.rem(c + j, ctx), t),
                device_id_type=MESH,
            ).start()

    rows_moved(0, seq - own, far_recv.at[0])

    q_copy.wait()

    @pl.when(s == 0)
    def _():
        pltpu.make_async_copy(base, base, in_sem.at[1]).wait()

    def place(i, at):
        return pl.ds(pl.multiple_of(i * width + at * chunk, chunk), chunk)

    def finish(at):
        cols = pl.ds(pl.multiple_of(at * chunk, chunk), chunk)
        landed = rbuf.at[pl.ds(0, tp - 1), :, cols]
        pltpu.make_async_copy(landed, landed, a_recv.at[at]).wait()

        @pl.when(s > 0)
        def _():
            arrived = base.at[:, :, cols]
            pltpu.make_async_copy(arrived, arrived, h_recv.at[at]).wait()

        @pl.loop(0, tp)
        def _(i):
            out_ref[:, place(i, at)] = (
                base[i, :, cols].astype(jnp.float32) + rbuf[i, :, cols].astype(jnp.float32)
            ).astype(jnp.bfloat16)

            @pl.when(s < sections - 1)
            def _():
                pltpu.make_async_remote_copy(
                    src_ref=out_ref.at[:, place(i, at)],
                    dst_ref=base.at[i, :, cols],
                    send_sem=h_send,
                    recv_sem=h_recv.at[at],
                    device_id=(lax.rem(s + 1, sections), c, t),
                    device_id_type=MESH,
                ).start()

    lag = chunks // 2 + s
    turn = TURN

    def share(first, count, at):
        cols = pl.ds(pl.multiple_of(first * HEAD_DIM, HEAD_DIM), count * HEAD_DIM)

        @pl.loop(1, tp)
        def _(j):
            pt = peer(tp - j)
            pltpu.make_async_remote_copy(
                src_ref=att.at[pl.ds(pl.multiple_of(pt * own, own), own), cols],
                dst_ref=rbuf.at[t, :, cols],
                send_sem=a_send,
                recv_sem=a_recv.at[at],
                device_id=(s, c, pt),
                device_id_type=MESH,
            ).start()

    def attend(g, n, stride):
        at = g * chunks_per_kv + n

        def head(h):
            return pl.ds(pl.multiple_of(at * chunk + h * HEAD_DIM, HEAD_DIM), HEAD_DIM)

        def dots(h):
            return lax.dot_general(
                q_buf[:, head(h)],
                kvbuf[g, :, pl.ds(0, HEAD_DIM)],
                (((1,), (1,)), ((), ())),
                preferred_element_type=jnp.float32,
            )

        following = dots(0)
        for h in range(chunk_heads):
            scores = following * SCORE_SCALE + bias[...]
            if h + 1 < chunk_heads:
                following = dots(h + 1)
            top = jnp.max(scores, axis=1, keepdims=True)
            weights = jnp.exp2(scores - top).astype(jnp.bfloat16)
            sums = jnp.dot(
                weights,
                kvbuf[g, :, pl.ds(HEAD_DIM, pair)],
                preferred_element_type=jnp.float32,
            )
            att[:, head(h)] = (sums[:, :HEAD_DIM] / sums[:, HEAD_DIM:]).astype(jnp.bfloat16)
            if (h + 1) % stride == 0:
                share(at * chunk_heads + h + 1 - stride, stride, at)

        cols = pl.ds(pl.multiple_of(at * chunk, chunk), chunk)
        rbuf[t, :, cols] = att[pl.ds(pl.multiple_of(t * own, own), own), cols]

        @pl.when(at >= lag)
        def _():
            finish(at - lag)

    def next_keys(g):
        rows_moved(g, (tp - 1) * own, plane_recv.at[g])
        spread(g)

    for g in range(kv_local):
        if g > 0:
            rows_moved(g, seq - rows, far_recv.at[g])
        begin = 0
        if g == 0 and chunk_heads % FIRST == 0 and FIRST < chunk_heads:
            attend(g, 0, FIRST)
            begin = 1
            if g + 1 < kv_local:
                @pl.when(turn == 0)
                def _():
                    next_keys(g + 1)

        @pl.loop(begin, chunks_per_kv)
        def _(n):
            attend(g, n, chunk_heads)

            if g + 1 < kv_local:
                @pl.when(n == turn)
                def _():
                    next_keys(g + 1)

    @pl.loop(jnp.maximum(chunks - lag, 0), chunks)
    def _(at):
        finish(at)

    @pl.when(s < sections - 1)
    def _():
        pltpu.make_async_copy(base, base, h_send).wait()

    for g in range(1, kv_local):
        rows_moved(g, (tp - 1) * own, plane_send.at[g])
        rows_moved(g, seq - rows, far_send.at[g])

    sent = rbuf.at[pl.ds(0, tp - 1)]
    pltpu.make_async_copy(sent, sent, a_send).wait()


def body(queries, key_vectors, value_vectors, positions, residual):
    sections, ctx, tp = (lax.axis_size(name) for name in ("section", "ctx", "tp"))
    rows = queries.shape[1]
    own = key_vectors.shape[1]
    seq = positions.shape[0]
    local_heads = HEADS // tp
    kv_local = max(1, KV_HEADS // tp)
    chunk_heads = min(4, local_heads // kv_local)
    chunks = local_heads // chunk_heads
    width = local_heads * HEAD_DIM
    sizes = (sections, ctx, tp, rows, own, kv_local, local_heads, chunk_heads)
    half = jnp.bfloat16
    hbm_spec = pl.BlockSpec(memory_space=pltpu.HBM)
    vmem_spec = pl.BlockSpec(memory_space=pltpu.VMEM)
    dma = pltpu.SemaphoreType.DMA
    hidden = pl.pallas_call(
        functools.partial(kernel, sizes),
        out_shape=pltpu.VMEM((own, HEADS * HEAD_DIM), half),
        in_specs=[hbm_spec] * 5,
        out_specs=vmem_spec,
        scratch_shapes=[
            pltpu.VMEM((rows, width), half),
            pltpu.VMEM((1, seq), jnp.int32),
            pltpu.VMEM((kv_local, seq, 3 * HEAD_DIM), half),
            pltpu.VMEM((rows, seq), jnp.float32),
            pltpu.VMEM((rows, width), half),
            pltpu.VMEM((tp, own, width), half),
            pltpu.VMEM((tp, own, width), half),
            dma((4,)),
            dma((kv_local,)),
            dma((kv_local,)),
            dma((kv_local,)),
            dma((kv_local,)),
            pltpu.SemaphoreType.REGULAR,
            dma,
            dma((chunks,)),
            dma,
            dma((chunks,)),
        ],
        compiler_params=pltpu.CompilerParams(
            collective_id=0, has_side_effects=True, vmem_limit_bytes=61 * 1024 * 1024
        ),
    )(queries[0], key_vectors[0], value_vectors[0], positions[None, :], residual)
    return hidden[None]


def solution(mesh):
    in_specs = (
        P("section", "ctx", "tp"),
        P("section", ("ctx", "tp"), None),
        P("section", ("ctx", "tp"), None),
        P(),
        P(("ctx", "tp"), None),
    )
    out_specs = P("section", ("ctx", "tp"), None)
    return jax.shard_map(body, mesh=mesh, in_specs=in_specs, out_specs=out_specs, check_vma=False)
```

```python
import functools
import math

import jax
import jax.numpy as jnp
from jax import lax
from jax.experimental import pallas as pl
from jax.experimental.pallas import tpu as pltpu
from jax.sharding import PartitionSpec as P

HEADS = 128
KV_HEADS = 8
HEAD_DIM = 128
MESH = pl.DeviceIdType.MESH
SCORE_SCALE = math.log2(math.e) / math.sqrt(HEAD_DIM)
HIDE = -1e30
FIRST = 2
TURN = 1


def kernel(
    sizes,
    q_hbm,
    k_hbm,
    v_hbm,
    pos_hbm,
    res_hbm,
    out_ref,
    q_buf,
    pos_ref,
    kvbuf,
    bias,
    att,
    rbuf,
    base,
    in_sem,
    plane_send,
    plane_recv,
    far_send,
    far_recv,
    gate,
    a_send,
    a_recv,
    h_send,
    h_recv,
):
    sections, ctx, tp, rows, own, kv_local, local_heads, chunk_heads = sizes
    group_size = HEADS // KV_HEADS
    width = local_heads * HEAD_DIM
    chunk = chunk_heads * HEAD_DIM
    chunks = local_heads // chunk_heads
    chunks_per_kv = chunks // kv_local
    seq = rows * ctx
    s = lax.axis_index("section")
    c = lax.axis_index("ctx")
    t = lax.axis_index("tp")
    me = c * tp + t

    def peer(j):
        return t ^ j if tp & (tp - 1) == 0 else lax.rem(t + j, tp)

    own_rows = pl.ds(pl.multiple_of(me * own, own), own)
    pair = 2 * HEAD_DIM

    barrier = pltpu.get_barrier_semaphore()

    @pl.loop(1, ctx * tp)
    def _(i):
        pl.semaphore_signal(
            barrier, inc=1, device_id=(s, lax.rem(c + i // tp, ctx), peer(lax.rem(i, tp))), device_id_type=MESH
        )

    @pl.when(s > 0)
    def _():
        pl.semaphore_signal(barrier, inc=1, device_id=(s - 1, c, t), device_id_type=MESH)

    @pl.when(s < sections - 1)
    def _():
        pl.semaphore_signal(barrier, inc=1, device_id=(s + 1, c, t), device_id_type=MESH)

    pos_copy = pltpu.make_async_copy(pos_hbm, pos_ref, in_sem.at[3])
    pos_copy.start()
    q_copy = pltpu.make_async_copy(q_hbm, q_buf, in_sem.at[0])

    def res_copy(i):
        return pltpu.make_async_copy(
            res_hbm.at[:, pl.ds(pl.multiple_of(i * width, width), width)],
            base.at[i],
            in_sem.at[1],
        )

    def column(pt, g):
        head = pt * local_heads // group_size + g
        return pl.ds(pl.multiple_of(head * HEAD_DIM, HEAD_DIM), HEAD_DIM)

    inner = jnp.minimum(s, 1) + jnp.minimum(sections - 1 - s, 1)
    pl.semaphore_wait(barrier, ctx * tp - 1 + inner)

    second = lax.rem(s, 2) == 1

    def kv_parts(g, pt):
        for part, src in enumerate((k_hbm, v_hbm)):
            dst = kvbuf.at[g, own_rows, pl.ds(part * HEAD_DIM, HEAD_DIM)]
            yield src.at[:, column(pt, g)], dst

    def kv_send(g, pc, pt, send_sem, recv_sem):
        for src, dst in kv_parts(g, pt):
            pltpu.make_async_remote_copy(
                src_ref=src,
                dst_ref=dst,
                send_sem=send_sem,
                recv_sem=recv_sem,
                device_id=(s, pc, pt),
                device_id_type=MESH,
            ).start()

    def rows_moved(g, count, sem):
        moved = kvbuf.at[g, pl.ds(0, count), pl.ds(0, pair)]
        pltpu.make_async_copy(moved, moved, sem).wait()

    @pl.when(second)
    def _():
        pl.semaphore_wait(gate, 1)

    @pl.loop(1, tp)
    def _(i):
        kv_send(0, c, peer(i), far_send.at[0], far_recv.at[0])

    @pl.loop(0, ctx * tp)
    def _(i):
        k = lax.rem(i, ctx)
        pc = jnp.where(2 * c < ctx, jnp.where(k == 0, ctx - 1, k - 1), jnp.where(k == 0, 0, ctx - k))

        @pl.when(pc != c)
        def _():
            kv_send(0, pc, peer(i // ctx), far_send.at[0], far_recv.at[0])


    for g in range(1, kv_local):

        @pl.loop(1, tp)
        def _(i):
            kv_send(g, c, peer(i), plane_send.at[g], plane_recv.at[g])

    for g in range(kv_local):
        for src, dst in kv_parts(g, t):
            pltpu.make_async_copy(src, dst, in_sem.at[2]).start()

    q_copy.start()

    @pl.when(s == 0)
    def _():
        @pl.loop(0, tp)
        def _(i):
            res_copy(i).start()

    for g in range(kv_local):
        kvbuf[g, :, pl.ds(pair, HEAD_DIM)] = jnp.ones((seq, HEAD_DIM), jnp.bfloat16)

    pos_copy.wait()
    query_row = pos_ref[:, pl.ds(pl.multiple_of(c * rows, rows), rows)].astype(jnp.float32)
    query_pos = jnp.broadcast_to(query_row, (HEAD_DIM, rows)).T
    for i in range(seq // HEAD_DIM):
        cols = pl.ds(i * HEAD_DIM, HEAD_DIM)
        key_pos = pos_ref[:, cols].astype(jnp.float32)
        bias[:, cols] = jnp.where(key_pos <= query_pos, 0.0, HIDE)

    rows_moved(0, seq - own, far_send.at[0])

    @pl.when((lax.rem(s, 2) == 0) & (s < sections - 1))
    def _():
        pl.semaphore_signal(gate, inc=1, device_id=(lax.rem(s + 1, sections), c, t), device_id_type=MESH)

    own_moved = kvbuf.at[:, pl.ds(0, own), pl.ds(0, pair)]
    pltpu.make_async_copy(own_moved, own_moved, in_sem.at[2]).wait()

    def spread(g):
        block = kvbuf.at[g, pl.ds(pl.multiple_of(c * rows, rows), rows), pl.ds(0, pair)]

        @pl.loop(1, ctx)
        def _(j):
            pltpu.make_async_remote_copy(
                src_ref=block,
                dst_ref=block,
                send_sem=far_send.at[g],
                recv_sem=far_recv.at[g],
                device_id=(s, lax.rem(c + j, ctx), t),
                device_id_type=MESH,
            ).start()

    rows_moved(0, seq - own, far_recv.at[0])

    q_copy.wait()

    @pl.when(s == 0)
    def _():
        pltpu.make_async_copy(base, base, in_sem.at[1]).wait()

    def place(i, at):
        return pl.ds(pl.multiple_of(i * width + at * chunk, chunk), chunk)

    def finish(at):
        cols = pl.ds(pl.multiple_of(at * chunk, chunk), chunk)
        landed = rbuf.at[pl.ds(0, tp - 1), :, cols]
        pltpu.make_async_copy(landed, landed, a_recv.at[at]).wait()

        @pl.when(s > 0)
        def _():
            arrived = base.at[:, :, cols]
            pltpu.make_async_copy(arrived, arrived, h_recv.at[at]).wait()

        @pl.loop(0, tp)
        def _(i):
            out_ref[:, place(i, at)] = (
                base[i, :, cols].astype(jnp.float32) + rbuf[i, :, cols].astype(jnp.float32)
            ).astype(jnp.bfloat16)

            @pl.when(s < sections - 1)
            def _():
                pltpu.make_async_remote_copy(
                    src_ref=out_ref.at[:, place(i, at)],
                    dst_ref=base.at[i, :, cols],
                    send_sem=h_send,
                    recv_sem=h_recv.at[at],
                    device_id=(lax.rem(s + 1, sections), c, t),
                    device_id_type=MESH,
                ).start()

    turn = TURN

    def share(first, count, at):
        cols = pl.ds(pl.multiple_of(first * HEAD_DIM, HEAD_DIM), count * HEAD_DIM)

        @pl.loop(1, tp)
        def _(j):
            pt = peer(tp - j)
            pltpu.make_async_remote_copy(
                src_ref=att.at[pl.ds(pl.multiple_of(pt * own, own), own), cols],
                dst_ref=rbuf.at[t, :, cols],
                send_sem=a_send,
                recv_sem=a_recv.at[at],
                device_id=(s, c, pt),
                device_id_type=MESH,
            ).start()

    def attend(g, n, stride):
        at = g * chunks_per_kv + n

        def head(h):
            return pl.ds(pl.multiple_of(at * chunk + h * HEAD_DIM, HEAD_DIM), HEAD_DIM)

        def dots(h):
            return lax.dot_general(
                q_buf[:, head(h)],
                kvbuf[g, :, pl.ds(0, HEAD_DIM)],
                (((1,), (1,)), ((), ())),
                preferred_element_type=jnp.float32,
            )

        following = dots(0)
        for h in range(chunk_heads):
            scores = following * SCORE_SCALE + bias[...]
            if h + 1 < chunk_heads:
                following = dots(h + 1)
            top = jnp.max(scores, axis=1, keepdims=True)
            weights = jnp.exp2(scores - top).astype(jnp.bfloat16)
            sums = jnp.dot(
                weights,
                kvbuf[g, :, pl.ds(HEAD_DIM, pair)],
                preferred_element_type=jnp.float32,
            )
            att[:, head(h)] = (sums[:, :HEAD_DIM] / sums[:, HEAD_DIM:]).astype(jnp.bfloat16)
            if (h + 1) % stride == 0:
                share(at * chunk_heads + h + 1 - stride, stride, at)

        cols = pl.ds(pl.multiple_of(at * chunk, chunk), chunk)
        rbuf[t, :, cols] = att[pl.ds(pl.multiple_of(t * own, own), own), cols]

    def next_keys(g):
        rows_moved(g, (tp - 1) * own, plane_recv.at[g])
        spread(g)

    for g in range(kv_local):
        if g > 0:
            rows_moved(g, seq - rows, far_recv.at[g])
        begin = 0
        if g == 0 and chunk_heads % FIRST == 0 and FIRST < chunk_heads:
            attend(g, 0, FIRST)
            begin = 1
            if g + 1 < kv_local:
                @pl.when(turn == 0)
                def _():
                    next_keys(g + 1)

        @pl.loop(begin, chunks_per_kv)
        def _(n):
            attend(g, n, chunk_heads)

            if g + 1 < kv_local:
                @pl.when(n == turn)
                def _():
                    next_keys(g + 1)

    @pl.loop(0, chunks)
    def _(at):
        finish(at)

    @pl.when(s < sections - 1)
    def _():
        pltpu.make_async_copy(base, base, h_send).wait()

    for g in range(1, kv_local):
        rows_moved(g, (tp - 1) * own, plane_send.at[g])
        rows_moved(g, seq - rows, far_send.at[g])

    sent = rbuf.at[pl.ds(0, tp - 1)]
    pltpu.make_async_copy(sent, sent, a_send).wait()


def body(queries, key_vectors, value_vectors, positions, residual):
    sections, ctx, tp = (lax.axis_size(name) for name in ("section", "ctx", "tp"))
    rows = queries.shape[1]
    own = key_vectors.shape[1]
    seq = positions.shape[0]
    local_heads = HEADS // tp
    kv_local = max(1, KV_HEADS // tp)
    chunk_heads = min(4, local_heads // kv_local)
    chunks = local_heads // chunk_heads
    width = local_heads * HEAD_DIM
    sizes = (sections, ctx, tp, rows, own, kv_local, local_heads, chunk_heads)
    half = jnp.bfloat16
    hbm_spec = pl.BlockSpec(memory_space=pltpu.HBM)
    vmem_spec = pl.BlockSpec(memory_space=pltpu.VMEM)
    dma = pltpu.SemaphoreType.DMA
    hidden = pl.pallas_call(
        functools.partial(kernel, sizes),
        out_shape=pltpu.VMEM((own, HEADS * HEAD_DIM), half),
        in_specs=[hbm_spec] * 5,
        out_specs=vmem_spec,
        scratch_shapes=[
            pltpu.VMEM((rows, width), half),
            pltpu.VMEM((1, seq), jnp.int32),
            pltpu.VMEM((kv_local, seq, 3 * HEAD_DIM), half),
            pltpu.VMEM((rows, seq), jnp.float32),
            pltpu.VMEM((rows, width), half),
            pltpu.VMEM((tp, own, width), half),
            pltpu.VMEM((tp, own, width), half),
            dma((4,)),
            dma((kv_local,)),
            dma((kv_local,)),
            dma((kv_local,)),
            dma((kv_local,)),
            pltpu.SemaphoreType.REGULAR,
            dma,
            dma((chunks,)),
            dma,
            dma((chunks,)),
        ],
        compiler_params=pltpu.CompilerParams(
            collective_id=0, has_side_effects=True, vmem_limit_bytes=61 * 1024 * 1024
        ),
    )(queries[0], key_vectors[0], value_vectors[0], positions[None, :], residual)
    return hidden[None]


def solution(mesh):
    in_specs = (
        P("section", "ctx", "tp"),
        P("section", ("ctx", "tp"), None),
        P("section", ("ctx", "tp"), None),
        P(),
        P(("ctx", "tp"), None),
    )
    out_specs = P("section", ("ctx", "tp"), None)
    return jax.shard_map(body, mesh=mesh, in_specs=in_specs, out_specs=out_specs, check_vma=False)
```

```python
import functools
import math

import jax
import jax.numpy as jnp
from jax import lax
from jax.experimental import pallas as pl
from jax.experimental.pallas import tpu as pltpu
from jax.sharding import PartitionSpec as P

HEADS = 128
KV_HEADS = 8
HEAD_DIM = 128
MESH = pl.DeviceIdType.MESH
SCORE_SCALE = math.log2(math.e) / math.sqrt(HEAD_DIM)
HIDE = -1e30
FIRST = 2
TURN = 1


def kernel(
    sizes,
    q_hbm,
    k_hbm,
    v_hbm,
    pos_hbm,
    res_hbm,
    out_ref,
    q_buf,
    pos_ref,
    kvbuf,
    bias,
    att,
    rbuf,
    base,
    in_sem,
    plane_send,
    plane_recv,
    far_send,
    far_recv,
    gate,
    a_send,
    a_recv,
    h_send,
    h_recv,
):
    sections, ctx, tp, rows, own, kv_local, local_heads, chunk_heads = sizes
    group_size = HEADS // KV_HEADS
    width = local_heads * HEAD_DIM
    chunk = chunk_heads * HEAD_DIM
    chunks = local_heads // chunk_heads
    chunks_per_kv = chunks // kv_local
    seq = rows * ctx
    s = lax.axis_index("section")
    c = lax.axis_index("ctx")
    t = lax.axis_index("tp")
    me = c * tp + t

    def peer(j):
        return t ^ j if tp & (tp - 1) == 0 else lax.rem(t + j, tp)

    own_rows = pl.ds(pl.multiple_of(me * own, own), own)
    pair = 2 * HEAD_DIM

    barrier = pltpu.get_barrier_semaphore()

    @pl.loop(1, ctx * tp)
    def _(i):
        pl.semaphore_signal(
            barrier, inc=1, device_id=(s, lax.rem(c + i // tp, ctx), peer(lax.rem(i, tp))), device_id_type=MESH
        )

    @pl.when(s > 0)
    def _():
        pl.semaphore_signal(barrier, inc=1, device_id=(s - 1, c, t), device_id_type=MESH)

    @pl.when(s < sections - 1)
    def _():
        pl.semaphore_signal(barrier, inc=1, device_id=(s + 1, c, t), device_id_type=MESH)

    pos_copy = pltpu.make_async_copy(pos_hbm, pos_ref, in_sem.at[3])
    pos_copy.start()
    q_copy = pltpu.make_async_copy(q_hbm, q_buf, in_sem.at[0])

    def res_copy(i):
        return pltpu.make_async_copy(
            res_hbm.at[:, pl.ds(pl.multiple_of(i * width, width), width)],
            base.at[i],
            in_sem.at[1],
        )

    def column(pt, g):
        head = pt * local_heads // group_size + g
        return pl.ds(pl.multiple_of(head * HEAD_DIM, HEAD_DIM), HEAD_DIM)

    inner = jnp.minimum(s, 1) + jnp.minimum(sections - 1 - s, 1)
    pl.semaphore_wait(barrier, ctx * tp - 1 + inner)

    second = lax.rem(s, 2) == 1

    def kv_parts(g, pt):
        for part, src in enumerate((k_hbm, v_hbm)):
            dst = kvbuf.at[g, own_rows, pl.ds(part * HEAD_DIM, HEAD_DIM)]
            yield src.at[:, column(pt, g)], dst

    def kv_send(g, pc, pt, send_sem, recv_sem):
        for src, dst in kv_parts(g, pt):
            pltpu.make_async_remote_copy(
                src_ref=src,
                dst_ref=dst,
                send_sem=send_sem,
                recv_sem=recv_sem,
                device_id=(s, pc, pt),
                device_id_type=MESH,
            ).start()

    def rows_moved(g, count, sem):
        moved = kvbuf.at[g, pl.ds(0, count), pl.ds(0, pair)]
        pltpu.make_async_copy(moved, moved, sem).wait()

    @pl.when(second)
    def _():
        for g in range(1, kv_local):

            @pl.loop(1, tp)
            def _(i):
                kv_send(g, c, peer(i), plane_send.at[g], plane_recv.at[g])

    @pl.when(second)
    def _():
        pl.semaphore_wait(gate, 1)

    @pl.loop(1, tp)
    def _(i):
        kv_send(0, c, peer(i), far_send.at[0], far_recv.at[0])

    @pl.loop(0, ctx * tp)
    def _(i):
        k = lax.rem(i, ctx)
        pc = jnp.where(2 * c < ctx, jnp.where(k == 0, ctx - 1, k - 1), jnp.where(k == 0, 0, ctx - k))

        @pl.when(pc != c)
        def _():
            kv_send(0, pc, peer(i // ctx), far_send.at[0], far_recv.at[0])


    @pl.when(jnp.logical_not(second))
    def _():
        for g in range(1, kv_local):

            @pl.loop(1, tp)
            def _(i):
                kv_send(g, c, peer(i), plane_send.at[g], plane_recv.at[g])

    for g in range(kv_local):
        for src, dst in kv_parts(g, t):
            pltpu.make_async_copy(src, dst, in_sem.at[2]).start()

    q_copy.start()

    @pl.when(s == 0)
    def _():
        @pl.loop(0, tp)
        def _(i):
            res_copy(i).start()

    for g in range(kv_local):
        kvbuf[g, :, pl.ds(pair, HEAD_DIM)] = jnp.ones((seq, HEAD_DIM), jnp.bfloat16)

    pos_copy.wait()
    query_row = pos_ref[:, pl.ds(pl.multiple_of(c * rows, rows), rows)].astype(jnp.float32)
    query_pos = jnp.broadcast_to(query_row, (HEAD_DIM, rows)).T
    for i in range(seq // HEAD_DIM):
        cols = pl.ds(i * HEAD_DIM, HEAD_DIM)
        key_pos = pos_ref[:, cols].astype(jnp.float32)
        bias[:, cols] = jnp.where(key_pos <= query_pos, 0.0, HIDE)

    rows_moved(0, seq - own, far_send.at[0])

    @pl.when((lax.rem(s, 2) == 0) & (s < sections - 1))
    def _():
        pl.semaphore_signal(gate, inc=1, device_id=(lax.rem(s + 1, sections), c, t), device_id_type=MESH)

    own_moved = kvbuf.at[:, pl.ds(0, own), pl.ds(0, pair)]
    pltpu.make_async_copy(own_moved, own_moved, in_sem.at[2]).wait()

    def spread(g):
        block = kvbuf.at[g, pl.ds(pl.multiple_of(c * rows, rows), rows), pl.ds(0, pair)]

        @pl.loop(1, ctx)
        def _(j):
            pltpu.make_async_remote_copy(
                src_ref=block,
                dst_ref=block,
                send_sem=far_send.at[g],
                recv_sem=far_recv.at[g],
                device_id=(s, lax.rem(c + j, ctx), t),
                device_id_type=MESH,
            ).start()

    rows_moved(0, seq - own, far_recv.at[0])

    q_copy.wait()

    @pl.when(s == 0)
    def _():
        pltpu.make_async_copy(base, base, in_sem.at[1]).wait()

    def place(i, at):
        return pl.ds(pl.multiple_of(i * width + at * chunk, chunk), chunk)

    def finish(at):
        cols = pl.ds(pl.multiple_of(at * chunk, chunk), chunk)
        landed = rbuf.at[pl.ds(0, tp - 1), :, cols]
        pltpu.make_async_copy(landed, landed, a_recv.at[at]).wait()

        @pl.when(s > 0)
        def _():
            arrived = base.at[:, :, cols]
            pltpu.make_async_copy(arrived, arrived, h_recv.at[at]).wait()

        @pl.loop(0, tp)
        def _(i):
            out_ref[:, place(i, at)] = (
                base[i, :, cols].astype(jnp.float32) + rbuf[i, :, cols].astype(jnp.float32)
            ).astype(jnp.bfloat16)

            @pl.when(s < sections - 1)
            def _():
                pltpu.make_async_remote_copy(
                    src_ref=out_ref.at[:, place(i, at)],
                    dst_ref=base.at[i, :, cols],
                    send_sem=h_send,
                    recv_sem=h_recv.at[at],
                    device_id=(lax.rem(s + 1, sections), c, t),
                    device_id_type=MESH,
                ).start()

    turn = TURN

    def share(first, count, at):
        cols = pl.ds(pl.multiple_of(first * HEAD_DIM, HEAD_DIM), count * HEAD_DIM)

        @pl.loop(1, tp)
        def _(j):
            pt = peer(tp - j)
            pltpu.make_async_remote_copy(
                src_ref=att.at[pl.ds(pl.multiple_of(pt * own, own), own), cols],
                dst_ref=rbuf.at[t, :, cols],
                send_sem=a_send,
                recv_sem=a_recv.at[at],
                device_id=(s, c, pt),
                device_id_type=MESH,
            ).start()

    def attend(g, n, stride):
        at = g * chunks_per_kv + n

        def head(h):
            return pl.ds(pl.multiple_of(at * chunk + h * HEAD_DIM, HEAD_DIM), HEAD_DIM)

        def dots(h):
            return lax.dot_general(
                q_buf[:, head(h)],
                kvbuf[g, :, pl.ds(0, HEAD_DIM)],
                (((1,), (1,)), ((), ())),
                preferred_element_type=jnp.float32,
            )

        following = dots(0)
        for h in range(chunk_heads):
            scores = following * SCORE_SCALE + bias[...]
            if h + 1 < chunk_heads:
                following = dots(h + 1)
            top = jnp.max(scores, axis=1, keepdims=True)
            weights = jnp.exp2(scores - top).astype(jnp.bfloat16)
            sums = jnp.dot(
                weights,
                kvbuf[g, :, pl.ds(HEAD_DIM, pair)],
                preferred_element_type=jnp.float32,
            )
            att[:, head(h)] = (sums[:, :HEAD_DIM] / sums[:, HEAD_DIM:]).astype(jnp.bfloat16)
            if (h + 1) % stride == 0:
                share(at * chunk_heads + h + 1 - stride, stride, at)

        cols = pl.ds(pl.multiple_of(at * chunk, chunk), chunk)
        rbuf[t, :, cols] = att[pl.ds(pl.multiple_of(t * own, own), own), cols]

    def next_keys(g):
        rows_moved(g, (tp - 1) * own, plane_recv.at[g])
        spread(g)

    for g in range(kv_local):
        if g > 0:
            rows_moved(g, seq - rows, far_recv.at[g])
        begin = 0
        if g == 0 and chunk_heads % FIRST == 0 and FIRST < chunk_heads:
            attend(g, 0, FIRST)
            begin = 1
            if g + 1 < kv_local:
                @pl.when(turn == 0)
                def _():
                    next_keys(g + 1)

        @pl.loop(begin, chunks_per_kv)
        def _(n):
            attend(g, n, chunk_heads)

            if g + 1 < kv_local:
                @pl.when(n == turn)
                def _():
                    next_keys(g + 1)

    @pl.loop(0, chunks)
    def _(at):
        finish(at)

    @pl.when(s < sections - 1)
    def _():
        pltpu.make_async_copy(base, base, h_send).wait()

    for g in range(1, kv_local):
        rows_moved(g, (tp - 1) * own, plane_send.at[g])
        rows_moved(g, seq - rows, far_send.at[g])

    sent = rbuf.at[pl.ds(0, tp - 1)]
    pltpu.make_async_copy(sent, sent, a_send).wait()


def body(queries, key_vectors, value_vectors, positions, residual):
    sections, ctx, tp = (lax.axis_size(name) for name in ("section", "ctx", "tp"))
    rows = queries.shape[1]
    own = key_vectors.shape[1]
    seq = positions.shape[0]
    local_heads = HEADS // tp
    kv_local = max(1, KV_HEADS // tp)
    chunk_heads = min(4, local_heads // kv_local)
    chunks = local_heads // chunk_heads
    width = local_heads * HEAD_DIM
    sizes = (sections, ctx, tp, rows, own, kv_local, local_heads, chunk_heads)
    half = jnp.bfloat16
    hbm_spec = pl.BlockSpec(memory_space=pltpu.HBM)
    vmem_spec = pl.BlockSpec(memory_space=pltpu.VMEM)
    dma = pltpu.SemaphoreType.DMA
    hidden = pl.pallas_call(
        functools.partial(kernel, sizes),
        out_shape=pltpu.VMEM((own, HEADS * HEAD_DIM), half),
        in_specs=[hbm_spec] * 5,
        out_specs=vmem_spec,
        scratch_shapes=[
            pltpu.VMEM((rows, width), half),
            pltpu.VMEM((1, seq), jnp.int32),
            pltpu.VMEM((kv_local, seq, 3 * HEAD_DIM), half),
            pltpu.VMEM((rows, seq), jnp.float32),
            pltpu.VMEM((rows, width), half),
            pltpu.VMEM((tp, own, width), half),
            pltpu.VMEM((tp, own, width), half),
            dma((4,)),
            dma((kv_local,)),
            dma((kv_local,)),
            dma((kv_local,)),
            dma((kv_local,)),
            pltpu.SemaphoreType.REGULAR,
            dma,
            dma((chunks,)),
            dma,
            dma((chunks,)),
        ],
        compiler_params=pltpu.CompilerParams(
            collective_id=0, has_side_effects=True, vmem_limit_bytes=61 * 1024 * 1024
        ),
    )(queries[0], key_vectors[0], value_vectors[0], positions[None, :], residual)
    return hidden[None]


def solution(mesh):
    in_specs = (
        P("section", "ctx", "tp"),
        P("section", ("ctx", "tp"), None),
        P("section", ("ctx", "tp"), None),
        P(),
        P(("ctx", "tp"), None),
    )
    out_specs = P("section", ("ctx", "tp"), None)
    return jax.shard_map(body, mesh=mesh, in_specs=in_specs, out_specs=out_specs, check_vma=False)
```
